32 devices in a mesh: ab: 4 (over y, x), cd: 4 (over z), ij: 2 (over core).
Axes of the slice: x: 2, y: 2, z: 4, core: 2. Of those that a mesh axis runs over, the one named last changes fastest.
Arguments:
- amplitudes: float32 [512, 4096], P('ij', ('cd', 'ab')), may hold values from -6 to 6
- integrals: float32 [256, 256, 256], P(('ab', 'cd')), may hold values from -0.375 to 0.375
- tile_row: int32 [256], P(('ab', 'cd')), may hold values from 0 to 3, as said below
- tile_col: int32 [256], P(('ab', 'cd')), may hold values from 0 to 3
- tile_count: int32 [16], P(('ab', 'cd')), may hold values from 1 to 16, as said below
Outputs:
- residual: float32 [512, 4, 16, 64], P('ij', 'ab', 'cd')
The draws below stay inside these ranges and needn't reach their ends.
Inputs may be any that keep to these rules, and one draw needn't show every extreme that they name: Within one slab the 16 slots name distinct (tile_row, tile_col) pairs. `tile_count`: in every draw some slab has all 16 slots live.
All inputs are finite; a program needn't handle non-finite values.
Results may differ from the reference program's by a relative error of at most 0.0003.
Values sent between devices are 32-bit elements; how exact they have to be, the bound alone decides.
A program may use at most 128 MiB of HBM per device.

```python
import jax
import jax.numpy as jnp
from jax import lax

OCC_DEV = 256
BS = 16
TS = 256
NBS = 4
OCC = 512
CT_DEV = 4
KT = 16
SLABS = 16
N_AB = 4
N_CD = 4


def tile_pairs(key):
    keys = jax.random.split(jax.random.fold_in(key, 11), SLABS)
    chosen = jax.vmap(lambda one_key: jax.random.permutation(one_key, NBS * CT_DEV)[:KT])(keys)
    return chosen.reshape(-1).astype(jnp.int32)


def draw_tile_row(key, part):
    return (tile_pairs(key) // CT_DEV).astype(jnp.int32)


def draw_tile_col(key, part):
    return (tile_pairs(key) % CT_DEV).astype(jnp.int32)


def draw_tile_count(key, part):
    counts = jax.random.randint(jax.random.fold_in(key, 5), (SLABS,), 1, KT + 1)
    fullest = jax.random.randint(jax.random.fold_in(key, 6), (), 0, SLABS)
    return counts.at[fullest].set(KT).astype(jnp.int32)


def level_of(rng, extent, pieces, smallest, high):
    level = 1.0
    for dim, shards_of in pieces:
        draws = jax.random.uniform(jax.random.fold_in(jax.random.fold_in(rng, 6), dim), (shards_of,), jnp.float32, smallest / len(pieces), high / len(pieces))
        level = level * jnp.repeat(jnp.exp(draws), extent[dim] // shards_of).reshape((-1,) + (1,) * (len(extent) - 1 - dim))
    return level


def gaussian(stream_key, shape, deviation, limit, cuts=(), kind=jnp.bfloat16):
    result = deviation * jax.random.normal(stream_key, shape, jnp.float32)
    if cuts:
        result = result * level_of(stream_key, shape, cuts, -0.22, 0.18)
    return jnp.clip(result, -limit, limit).astype(kind)


def setup_inputs(seed: int = 0) -> dict:
    key_of = jax.random.split(jax.random.key(seed), 6)
    amplitudes = gaussian(key_of[0], (OCC, N_AB * N_AB * TS), 1.0, 6.0, ((0, 2), (1, 16)), jnp.float32)
    integrals = gaussian(key_of[1], (SLABS * KT, TS, TS), TS ** -0.5, 0.375, ((0, 16),), jnp.float32)
    tile_row = draw_tile_row(jax.random.fold_in(key_of[5], 71), 0)
    tile_col = draw_tile_col(jax.random.fold_in(key_of[5], 71), 0)
    tile_count = draw_tile_count(jax.random.fold_in(key_of[5], 71), 0)
    return {"amplitudes": amplitudes, "integrals": integrals, "tile_row": tile_row, "tile_col": tile_col, "tile_count": tile_count}


def reference(amplitudes, integrals, tile_row, tile_col, tile_count):
    amp_tiles = amplitudes.reshape(OCC, N_AB * N_AB, TS)
    slab_tiles = integrals.reshape(SLABS, KT, TS, TS)
    slab_rows = tile_row.reshape(SLABS, KT)
    slab_cols = tile_col.reshape(SLABS, KT)
    slab_ids = jnp.arange(SLABS, dtype=jnp.int32)

    def add_slab(total, item):
        slab_id, tiles, rows, cols, live_count = item
        ab_index = slab_id // N_CD
        cd_index = slab_id % N_CD
        chosen = jnp.take(amp_tiles, (cd_index * CT_DEV + cols).astype(jnp.int32), axis=1)
        terms = jnp.einsum("okf,kef->oke", chosen, tiles, precision=lax.Precision.HIGHEST)
        live = (jnp.arange(KT, dtype=jnp.int32) < live_count).astype(jnp.float32)
        terms = terms * live[None, :, None]
        total = total.at[:, (ab_index * NBS + rows).astype(jnp.int32), :].add(terms)
        return total, None

    start = jnp.zeros((OCC, NBS * NBS, TS), jnp.float32)
    ladder, _ = lax.scan(add_slab, start, (slab_ids, slab_tiles, slab_rows, slab_cols, tile_count))
    ladder_five = ladder.reshape(OCC, NBS, NBS, BS, BS)
    partner = jnp.roll(ladder_five, OCC_DEV, axis=0)
    mirrored = jnp.transpose(partner, (0, 2, 1, 4, 3))
    total = ladder_five + mirrored
    return jnp.transpose(total, (0, 1, 3, 2, 4)).reshape(OCC, NBS, BS, NBS * BS)
```

```python
import functools
import math

import jax
import jax.numpy as jnp
from jax import lax
from jax.experimental import pallas as pl
from jax.experimental.pallas import tpu as pltpu
from jax.sharding import PartitionSpec as P

MESH = pl.DeviceIdType.MESH
LANES = 128
VMEM_BYTES = 63 * 1024 * 1024


def split(value):
    high = value.astype(jnp.bfloat16)
    low = (value - high.astype(jnp.float32)).astype(jnp.bfloat16)
    return high, low


def ladder_kernel(
    n_ab, n_cd, block,
    row_ref, col_ref, count_ref, amp_ref, tiles_ref, out_ref,
    tiles, w_high, w_low, gathered, a_both, partial, mirror_out, mirror_in, z_in, relayed,
    summed, outgoing, mirrored, result, traded,
    tile_sem, own_sem, ag_send, ag_recv, x_send, x_recv, z_send, z_recv,
    mi_send, mi_recv, tr_send, tr_recv,
):
    me_ab, me_cd, me_ij = lax.axis_index("ab"), lax.axis_index("cd"), lax.axis_index("ij")
    slots, size = tiles_ref.shape[0], tiles_ref.shape[1]
    steps = partial.shape[0]
    half = LANES // 2
    group = block // n_cd
    width = n_ab * block
    rows = group * width
    targets = n_ab * n_cd
    piece = group * group
    own_place = me_ab * n_cd + me_cd
    near = [me_ab, me_ab + 1 - 2 * lax.rem(me_ab, 2), lax.rem(me_ab + 2, n_ab), n_ab - 1 - me_ab]
    low_side = me_cd < n_cd // 2
    outer = (me_cd == 0) | (me_cd == n_cd - 1)
    inner = (me_cd > 0) & (me_cd < n_cd - 1)
    far = jnp.where(low_side, n_cd - 1, 0)
    next_in = jnp.where(low_side, 1, 2)
    order = [
        far,
        jnp.where(outer, n_cd - 1 - next_in, n_cd - 1 - far),
        jnp.where(outer, next_in, n_cd - 1 - me_cd),
        me_cd,
    ]
    z_device = [
        far,
        jnp.where(outer, next_in, n_cd - 1 - far),
        jnp.where(outer, next_in, n_cd - 1 - me_cd),
    ]
    z_slot = [jnp.where(outer, 0, 2), jnp.where(outer, 3, 1), jnp.where(outer, 0, 1)]

    tile_copies = [
        pltpu.make_async_copy(tiles_ref.at[k], tiles.at[k], tile_sem.at[k]) for k in range(slots)
    ]
    for copy in tile_copies:
        copy.start()

    barrier = pltpu.get_barrier_semaphore()
    for j in range(1, n_ab):
        for core in range(2):
            pl.semaphore_signal(
                barrier, inc=1, device_id=(near[j], me_cd, core), device_id_type=MESH
            )
    pl.semaphore_signal(barrier, inc=1, device_id=(me_ab, me_cd, 1 - me_ij), device_id_type=MESH)
    for m in range(1, n_cd):
        pl.semaphore_signal(
            barrier, inc=1, device_id=(me_ab, lax.rem(me_cd + m, n_cd), me_ij), device_id_type=MESH
        )
    pl.semaphore_wait(barrier, 2 * (n_ab - 1) + 1 + n_cd - 1)

    def spread(s, core, j):
        return pltpu.make_async_remote_copy(
            src_ref=amp_ref.at[pl.ds((2 * s + core) * half, half)],
            dst_ref=gathered.at[s, j, pl.ds(me_ij * half, half)],
            send_sem=ag_send.at[s, core, j],
            recv_sem=ag_recv.at[s, j, me_ij],
            device_id=(near[j], me_cd, core),
            device_id_type=MESH,
        )

    def arrival(s, j, h):
        return pltpu.make_async_remote_copy(
            src_ref=amp_ref.at[pl.ds(0, half)],
            dst_ref=gathered.at[s, j, pl.ds(h * half, half)],
            send_sem=ag_send.at[s, 0, j],
            recv_sem=ag_recv.at[s, j, h],
            device_id=(near[j], me_cd, me_ij),
            device_id_type=MESH,
        )

    def keep(s, core):
        return pltpu.make_async_copy(
            amp_ref.at[pl.ds((2 * s + core) * half, half)],
            gathered.at[s, 0, pl.ds(core * half, half)],
            own_sem.at[s],
        )

    for s in range(steps):
        for core in range(2):
            for j in (3, 1, 2):
                spread(s, core, j).start()

            @pl.when(me_ij == core)
            def _():
                keep(s, core).start()

            @pl.when(me_ij != core)
            def _():
                spread(s, core, 0).start()

    keys = [row_ref[k] * n_ab + col_ref[k] for k in range(slots)]
    live_count = count_ref[0]
    for copy in tile_copies:
        copy.wait()
    for j in range(n_ab):
        column = near[j]
        for r in range(n_ab):
            slot = jnp.int32(0)
            for k in range(1, slots):
                slot = jnp.where(keys[k] == r * n_ab + column, jnp.int32(k), slot)
            scale = jnp.where(slot < live_count, jnp.float32(1), jnp.float32(0))
            high, low = split(tiles[slot] * scale)
            at = (slice(None), pl.ds(r * block, block), pl.ds(j * size, size))
            w_high[at] = high.reshape(block, block, size)
            w_low[at] = low.reshape(block, block, size)

    contract = (((1,), (1,)), ((), ()))

    def to_plane(s, i):
        source = partial.at[s, pl.ds(order[i] * rows, rows)]
        return pltpu.make_async_remote_copy(
            src_ref=source,
            dst_ref=z_in.at[s, z_slot[i]],
            send_sem=z_send.at[s, i],
            recv_sem=z_recv.at[s, z_slot[i]],
            device_id=(me_ab, z_device[i], me_ij),
            device_id_type=MESH,
        )

    def passed_on(s):
        return pltpu.make_async_remote_copy(
            src_ref=relayed.at[s],
            dst_ref=z_in.at[s, 1],
            send_sem=z_send.at[s, 2],
            recv_sem=z_recv.at[s, 1],
            device_id=(me_ab, z_device[2], me_ij),
            device_id_type=MESH,
        )

    def from_plane(s, place):
        return pltpu.make_async_remote_copy(
            src_ref=relayed.at[s],
            dst_ref=z_in.at[s, place],
            send_sem=z_send.at[s, 0],
            recv_sem=z_recv.at[s, place],
            device_id=(me_ab, z_device[0], me_ij),
            device_id_type=MESH,
        )

    def send_plane(s, i):
        if i < 2:
            to_plane(s, i).start()
        elif i == 2:

            @pl.when(outer)
            def _():
                to_plane(s, i).start()

    def gather(s):
        for j in range(n_ab):
            if j:
                arrival(s, j, 0).wait_recv()
                arrival(s, j, 1).wait_recv()
            else:

                @pl.when(me_ij == 0)
                def _():
                    keep(s, 0).wait()
                    arrival(s, 0, 1).wait_recv()

                @pl.when(me_ij == 1)
                def _():
                    keep(s, 1).wait()
                    arrival(s, 0, 0).wait_recv()

            high, low = split(gathered[s, j])
            a_both[pl.ds(0, LANES), pl.ds(j * size, size)] = high
            a_both[pl.ds(LANES, LANES), pl.ds(j * size, size)] = low

    def compute(s, send):
        for i in range(n_cd):
            d = order[i]
            lead = pl.ds(d * group, group)
            left_high = w_high[lead].reshape(rows, n_ab * size)
            left_low = w_low[lead].reshape(rows, n_ab * size)
            right = a_both[...]
            wide = lax.dot_general(left_high, right, contract, preferred_element_type=jnp.float32)
            value = wide[:, LANES:] + lax.dot_general(
                left_low, right[:LANES], contract, preferred_element_type=jnp.float32
            )
            value += wide[:, :LANES]
            partial[s, pl.ds(d * rows, rows)] = value
            if send:
                send_plane(s, i)
            else:
                for j in range(n_ab):
                    for x in range(group):
                        mirror_out[j, pl.ds(d * group + x, block, stride=block), :] = pltpu.roll(
                            partial[s, pl.ds(d * rows + x * width + near[j] * block, block)], half, 1
                        )

    def across(j, i):
        part = pl.ds(order[i] * group * block, group * block)
        return pltpu.make_async_remote_copy(
            src_ref=mirror_out.at[j, part],
            dst_ref=mirror_in.at[j, part],
            send_sem=x_send.at[j, i],
            recv_sem=x_recv.at[j, i],
            device_id=(near[j], me_cd, me_ij),
            device_id_type=MESH,
        )

    def add_mirrors(s):
        for i in range(n_cd):
            d = order[i]
            for j in range(n_ab):
                source = mirror_out if j == 0 else mirror_in
                if j:
                    across(j, i).wait_recv()
                for x in range(group):
                    at = pl.ds(d * rows + x * width + near[j] * block, block)
                    partial[s, at] += source[j, pl.ds((d * group + x) * block, block)]
            send_plane(s, i)

    def relay(s):
        @pl.when(inner)
        def _():
            from_plane(s, 3).wait_recv()
            relayed[s] = partial[s, pl.ds(order[2] * rows, rows)] + z_in[s, 3]
            passed_on(s).start()

    def total(s, into):
        from_plane(s, 0).wait_recv()
        from_plane(s, 1).wait_recv()
        into[s] = partial[s, pl.ds(me_cd * rows, rows)] + z_in[s, 0] + z_in[s, 1]

        @pl.when(outer)
        def _():
            from_plane(s, 2).wait_recv()
            into[s] += z_in[s, 2]

    def mirror_copy(s, j, m):
        q = lax.rem(me_cd + m, n_cd)
        return pltpu.make_async_remote_copy(
            src_ref=outgoing.at[s, pl.ds((near[j] * n_cd + q) * piece, piece)],
            dst_ref=mirrored.at[s, pl.ds(own_place * piece, piece)],
            send_sem=mi_send.at[s, j, m],
            recv_sem=mi_recv.at[s, j, m],
            device_id=(near[j], q, me_ij),
            device_id_type=MESH,
        )

    def mirror_arrival(s, j, m):
        place = near[j] * n_cd + lax.rem(me_cd - m + n_cd, n_cd)
        return pltpu.make_async_remote_copy(
            src_ref=outgoing.at[s, pl.ds(0, piece)],
            dst_ref=mirrored.at[s, pl.ds(place * piece, piece)],
            send_sem=mi_send.at[s, j, m],
            recv_sem=mi_recv.at[s, j, m],
            device_id=(near[j], lax.rem(me_cd + m, n_cd), me_ij),
            device_id_type=MESH,
        )

    others = [(j, m) for j in (3, 1, 2, 0) for m in (2, 3, 1, 0) if j or m]

    def send_mirrors(s):
        for x in range(group):
            for y in range(group):
                outgoing[s, pl.ds(x * group + y, targets, stride=piece), :] = pltpu.roll(
                    summed[s, pl.ds(x * width + y, targets, stride=group), :], half, 1
                )
        for j, m in others:
            mirror_copy(s, j, m).start()
        here = pl.ds(own_place * piece, piece)
        mirrored[s, here] = outgoing[s, here]

    def take_mirrors(s):
        for j, m in others:
            mirror_arrival(s, j, m).wait_recv()
        for y in range(group):
            at = pl.ds(y * width, width)
            result[s, at] = summed[s, at] + mirrored[s, pl.ds(y, width, stride=group), :]

    def trade(s):
        return pltpu.make_async_remote_copy(
            src_ref=result.at[s],
            dst_ref=traded.at[s],
            send_sem=tr_send.at[s],
            recv_sem=tr_recv.at[s],
            device_id=(me_ab, me_cd, 1 - me_ij),
            device_id_type=MESH,
        )

    def store(s):
        trade(s).wait_recv()
        lane = lax.broadcasted_iota(jnp.int32, (width, LANES), 1)
        mine = (lane >= half) == (me_ij == 1)
        for y in range(group):
            at = pl.ds(y * width, width)
            out_ref[y, :, pl.ds(s * LANES, LANES)] = jnp.where(
                mine, result[s, at], pltpu.roll(traded[s, at], half, 1)
            )

    last = steps - 1
    for s in range(last):
        gather(s)
        compute(s, True)
        relay(s)
    gather(last)
    compute(last, False)
    for i in range(n_cd):
        for j in (3, 1, 2):
            across(j, i).start()
    for s in range(last):
        total(s, summed)
        send_mirrors(s)
    add_mirrors(last)
    relay(last)
    for s in range(last):
        take_mirrors(s)
        trade(s).start()
    total(last, result)
    trade(last).start()
    for s in range(steps):
        store(s)

    for s in range(steps):
        trade(s).wait_send()
        for core in range(2):
            for j in range(1, n_ab):
                spread(s, core, j).wait_send()

            @pl.when(me_ij != core)
            def _():
                spread(s, core, 0).wait_send()

        for i in range(3):
            to_plane(s, i).wait_send()
    for i in range(n_cd):
        for j in range(1, n_ab):
            across(j, i).wait_send()
    for s in range(last):
        for j, m in others:
            mirror_copy(s, j, m).wait_send()


def fused(amplitudes, integrals, tile_row, tile_col, tile_count):
    occ_dev = amplitudes.shape[0]
    slots, size = integrals.shape[0], integrals.shape[1]
    block = math.isqrt(size)
    n_ab, n_cd = lax.axis_size("ab"), lax.axis_size("cd")
    group = block // n_cd
    rows = group * n_ab * block
    steps = occ_dev // LANES
    targets = n_ab * n_cd
    piece = group * group
    f32, bf16 = jnp.float32, jnp.bfloat16
    dma = pltpu.SemaphoreType.DMA
    out = pl.pallas_call(
        functools.partial(ladder_kernel, n_ab, n_cd, block),
        out_shape=jax.ShapeDtypeStruct((group, n_ab * block, occ_dev), f32),
        in_specs=[pl.BlockSpec(memory_space=pltpu.SMEM)] * 3
        + [pl.BlockSpec(memory_space=pl.ANY)] * 2,
        out_specs=pl.BlockSpec(memory_space=pltpu.VMEM),
        scratch_shapes=[
            pltpu.VMEM((slots, size, size), f32),
            pltpu.VMEM((block, n_ab * block, n_ab * size), bf16),
            pltpu.VMEM((block, n_ab * block, n_ab * size), bf16),
            pltpu.VMEM((steps, n_ab, LANES, size), f32),
            pltpu.VMEM((2 * LANES, n_ab * size), bf16),
            pltpu.VMEM((steps, n_cd * rows, LANES), f32),
            pltpu.VMEM((n_ab, size, LANES), f32),
            pltpu.VMEM((n_ab, size, LANES), f32),
            pltpu.VMEM((steps, 4, rows, LANES), f32),
            pltpu.VMEM((steps, rows, LANES), f32),
            pltpu.VMEM((steps, rows, LANES), f32),
            pltpu.VMEM((steps, targets * piece, LANES), f32),
            pltpu.VMEM((steps, targets * piece, LANES), f32),
            pltpu.VMEM((steps, rows, LANES), f32),
            pltpu.VMEM((steps, rows, LANES), f32),
            dma((slots,)),
            dma((steps,)),
            dma((steps, 2, n_ab)),
            dma((steps, n_ab, 2)),
            dma((n_ab, n_cd)),
            dma((n_ab, n_cd)),
            dma((steps, 3)),
            dma((steps, 4)),
            dma((steps, n_ab, n_cd)),
            dma((steps, n_ab, n_cd)),
            dma((steps,)),
            dma((steps,)),
        ],
        compiler_params=pltpu.CompilerParams(
            collective_id=0, has_side_effects=True, vmem_limit_bytes=VMEM_BYTES
        ),
    )(tile_row, tile_col, tile_count, amplitudes, integrals)
    return jnp.transpose(out, (2, 0, 1))[:, None]


def from_partner(block, axis, bit):
    count = lax.axis_size(axis)
    route = []
    for low in range(count):
        high = low | 1 << bit
        if high != low and high < count:
            route += [(low, high), (high, low)]
    return lax.ppermute(block, axis, route)


def place_rows(chosen, tile_rows, row_picks, block_size):
    terms = jnp.einsum("okf,kef->oke", chosen, tile_rows, precision=lax.Precision.HIGHEST)
    occ_dev, slots, width = terms.shape
    terms = terms.reshape(occ_dev, slots, width // block_size, block_size)
    placed = jnp.einsum("rk,okab->aorb", row_picks, terms, precision=lax.Precision.HIGHEST)
    return placed.reshape(width // block_size, occ_dev, row_picks.shape[0] * block_size)


def general(amplitudes, integrals, tile_row, tile_col, tile_count):
    occ_dev = amplitudes.shape[0]
    slots = integrals.shape[0]
    tile_size = integrals.shape[1]
    block_size = math.isqrt(tile_size)
    blocks = lax.axis_size("ab")
    cd_size = lax.axis_size("cd")
    group_size = block_size // cd_size
    live_count = tile_count[0]
    live = jnp.arange(slots, dtype=jnp.int32) < live_count
    row_picks = (
        (tile_row[None, :] == jnp.arange(blocks, dtype=jnp.int32)[:, None]) & live[None, :]
    ).astype(jnp.float32)
    gathered = lax.all_gather(amplitudes, "ab", axis=1, tiled=True)
    columns = gathered.reshape(occ_dev, -1, tile_size)
    chosen = jnp.take(columns, tile_col, axis=1)
    partial_value = place_rows(chosen, integrals, row_picks, block_size)
    summed = lax.psum_scatter(partial_value, "cd", scatter_dimension=0, tiled=True)
    direct = jnp.transpose(summed, (1, 0, 2))
    outgoing = summed.reshape(group_size, occ_dev, blocks, cd_size, group_size)
    outgoing = jnp.transpose(outgoing, (2, 3, 1, 0, 4))
    arrived = lax.all_to_all(
        outgoing.reshape(blocks * cd_size, occ_dev * group_size * group_size),
        ("ab", "cd"),
        split_axis=0,
        concat_axis=0,
        tiled=True,
    )
    arrived = arrived.reshape(blocks, cd_size, occ_dev, group_size, group_size)
    mirrored = jnp.transpose(arrived, (2, 4, 0, 1, 3)).reshape(
        occ_dev, group_size, blocks * block_size
    )
    partner = from_partner(mirrored, "ij", 0)
    return (direct + partner).reshape(occ_dev, 1, group_size, blocks * block_size)


def per_device(amplitudes, integrals, tile_row, tile_col, tile_count):
    n_ab = lax.axis_size("ab")
    if (
        amplitudes.shape[1] == integrals.shape[1]
        and integrals.shape[0] == n_ab * n_ab
        and n_ab == 4
        and lax.axis_size("cd") == 4
        and lax.axis_size("ij") == 2
        and amplitudes.shape[0] % LANES == 0
    ):
        return fused(amplitudes, integrals, tile_row, tile_col, tile_count)
    return general(amplitudes, integrals, tile_row, tile_col, tile_count)


def solution(mesh):
    in_specs = (
        P("ij", ("cd", "ab")),
        P(("ab", "cd"), None, None),
        P(("ab", "cd")),
        P(("ab", "cd")),
        P(("ab", "cd")),
    )
    out_specs = P("ij", "ab", "cd", None)
    return jax.shard_map(
        per_device, mesh=mesh, in_specs=in_specs, out_specs=out_specs, check_vma=False
    )
```

```python
import functools
import math

import jax
import jax.numpy as jnp
from jax import lax
from jax.experimental import pallas as pl
from jax.experimental.pallas import tpu as pltpu
from jax.sharding import PartitionSpec as P

MESH = pl.DeviceIdType.MESH
LANES = 128
VMEM_BYTES = 63 * 1024 * 1024


def split(value):
    high = value.astype(jnp.bfloat16)
    low = (value - high.astype(jnp.float32)).astype(jnp.bfloat16)
    return high, low


def ladder_kernel(
    n_ab, n_cd, block,
    row_ref, col_ref, count_ref, amp_ref, tiles_ref, out_ref,
    tiles, w_high, w_low, gathered, a_both, partial, mirror_out, mirror_in, z_in, relayed,
    summed, outgoing, mirrored, result, traded,
    tile_sem, own_sem, ag_send, ag_recv, x_send, x_recv, z_send, z_recv,
    mi_send, mi_recv, tr_send, tr_recv,
):
    me_ab, me_cd, me_ij = lax.axis_index("ab"), lax.axis_index("cd"), lax.axis_index("ij")
    slots, size = tiles_ref.shape[0], tiles_ref.shape[1]
    steps = partial.shape[0]
    half = LANES // 2
    group = block // n_cd
    width = n_ab * block
    rows = group * width
    targets = n_ab * n_cd
    piece = group * group
    own_place = me_ab * n_cd + me_cd
    near = [me_ab, me_ab + 1 - 2 * lax.rem(me_ab, 2), lax.rem(me_ab + 2, n_ab), n_ab - 1 - me_ab]
    low_side = me_cd < n_cd // 2
    outer = (me_cd == 0) | (me_cd == n_cd - 1)
    inner = (me_cd > 0) & (me_cd < n_cd - 1)
    far = jnp.where(low_side, n_cd - 1, 0)
    next_in = jnp.where(low_side, 1, 2)
    order = [
        jnp.where(outer, n_cd - 1 - next_in, far),
        jnp.where(outer, far, n_cd - 1 - far),
        jnp.where(outer, next_in, n_cd - 1 - me_cd),
        me_cd,
    ]
    z_device = [
        jnp.where(outer, next_in, far),
        jnp.where(outer, far, n_cd - 1 - far),
        jnp.where(outer, next_in, n_cd - 1 - me_cd),
    ]
    z_slot = [jnp.where(outer, 3, 2), jnp.where(outer, 0, 1), jnp.where(outer, 0, 1)]

    tile_copies = [
        pltpu.make_async_copy(tiles_ref.at[k], tiles.at[k], tile_sem.at[k]) for k in range(slots)
    ]
    for copy in tile_copies:
        copy.start()

    barrier = pltpu.get_barrier_semaphore()
    for j in range(1, n_ab):
        for core in range(2):
            pl.semaphore_signal(
                barrier, inc=1, device_id=(near[j], me_cd, core), device_id_type=MESH
            )
    pl.semaphore_signal(barrier, inc=1, device_id=(me_ab, me_cd, 1 - me_ij), device_id_type=MESH)
    for m in range(1, n_cd):
        pl.semaphore_signal(
            barrier, inc=1, device_id=(me_ab, lax.rem(me_cd + m, n_cd), me_ij), device_id_type=MESH
        )
    pl.semaphore_wait(barrier, 2 * (n_ab - 1) + 1 + n_cd - 1)

    def spread(s, core, j):
        return pltpu.make_async_remote_copy(
            src_ref=amp_ref.at[pl.ds((2 * s + core) * half, half)],
            dst_ref=gathered.at[s, j, pl.ds(me_ij * half, half)],
            send_sem=ag_send.at[s, core, j],
            recv_sem=ag_recv.at[s, j, me_ij],
            device_id=(near[j], me_cd, core),
            device_id_type=MESH,
        )

    def arrival(s, j, h):
        return pltpu.make_async_remote_copy(
            src_ref=amp_ref.at[pl.ds(0, half)],
            dst_ref=gathered.at[s, j, pl.ds(h * half, half)],
            send_sem=ag_send.at[s, 0, j],
            recv_sem=ag_recv.at[s, j, h],
            device_id=(near[j], me_cd, me_ij),
            device_id_type=MESH,
        )

    def keep(s, core):
        return pltpu.make_async_copy(
            amp_ref.at[pl.ds((2 * s + core) * half, half)],
            gathered.at[s, 0, pl.ds(core * half, half)],
            own_sem.at[s],
        )

    for s in range(steps):
        for core in range(2):
            for j in (3, 1, 2):
                spread(s, core, j).start()

            @pl.when(me_ij == core)
            def _():
                keep(s, core).start()

            @pl.when(me_ij != core)
            def _():
                spread(s, core, 0).start()

    keys = [row_ref[k] * n_ab + col_ref[k] for k in range(slots)]
    live_count = count_ref[0]
    for copy in tile_copies:
        copy.wait()
    for j in range(n_ab):
        column = near[j]
        for r in range(n_ab):
            slot = jnp.int32(0)
            for k in range(1, slots):
                slot = jnp.where(keys[k] == r * n_ab + column, jnp.int32(k), slot)
            scale = jnp.where(slot < live_count, jnp.float32(1), jnp.float32(0))
            high, low = split(tiles[slot] * scale)
            at = (slice(None), pl.ds(r * block, block), pl.ds(j * size, size))
            w_high[at] = high.reshape(block, block, size)
            w_low[at] = low.reshape(block, block, size)

    contract = (((1,), (1,)), ((), ()))

    def to_plane(s, i):
        source = partial.at[s, pl.ds(order[i] * rows, rows)]
        return pltpu.make_async_remote_copy(
            src_ref=source,
            dst_ref=z_in.at[s, z_slot[i]],
            send_sem=z_send.at[s, i],
            recv_sem=z_recv.at[s, z_slot[i]],
            device_id=(me_ab, z_device[i], me_ij),
            device_id_type=MESH,
        )

    def passed_on(s):
        return pltpu.make_async_remote_copy(
            src_ref=relayed.at[s],
            dst_ref=z_in.at[s, 1],
            send_sem=z_send.at[s, 2],
            recv_sem=z_recv.at[s, 1],
            device_id=(me_ab, z_device[2], me_ij),
            device_id_type=MESH,
        )

    def from_plane(s, place):
        return pltpu.make_async_remote_copy(
            src_ref=relayed.at[s],
            dst_ref=z_in.at[s, place],
            send_sem=z_send.at[s, 0],
            recv_sem=z_recv.at[s, place],
            device_id=(me_ab, z_device[0], me_ij),
            device_id_type=MESH,
        )

    def send_plane(s, i):
        if i < 2:
            to_plane(s, i).start()
        elif i == 2:

            @pl.when(outer)
            def _():
                to_plane(s, i).start()

    def gather(s):
        for j in range(n_ab):
            if j:
                arrival(s, j, 0).wait_recv()
                arrival(s, j, 1).wait_recv()
            else:

                @pl.when(me_ij == 0)
                def _():
                    keep(s, 0).wait()
                    arrival(s, 0, 1).wait_recv()

                @pl.when(me_ij == 1)
                def _():
                    keep(s, 1).wait()
                    arrival(s, 0, 0).wait_recv()

            high, low = split(gathered[s, j])
            a_both[pl.ds(0, LANES), pl.ds(j * size, size)] = high
            a_both[pl.ds(LANES, LANES), pl.ds(j * size, size)] = low

    def compute(s, send):
        for i in range(n_cd):
            d = order[i]
            lead = pl.ds(d * group, group)
            left_high = w_high[lead].reshape(rows, n_ab * size)
            left_low = w_low[lead].reshape(rows, n_ab * size)
            right = a_both[...]
            wide = lax.dot_general(left_high, right, contract, preferred_element_type=jnp.float32)
            value = wide[:, LANES:] + lax.dot_general(
                left_low, right[:LANES], contract, preferred_element_type=jnp.float32
            )
            value += wide[:, :LANES]
            partial[s, pl.ds(d * rows, rows)] = value
            if send:
                send_plane(s, i)
            else:
                for j in range(n_ab):
                    for x in range(group):
                        mirror_out[j, pl.ds(d * group + x, block, stride=block), :] = pltpu.roll(
                            partial[s, pl.ds(d * rows + x * width + near[j] * block, block)], half, 1
                        )

    def across(j, i):
        part = pl.ds(order[i] * group * block, group * block)
        return pltpu.make_async_remote_copy(
            src_ref=mirror_out.at[j, part],
            dst_ref=mirror_in.at[j, part],
            send_sem=x_send.at[j, i],
            recv_sem=x_recv.at[j, i],
            device_id=(near[j], me_cd, me_ij),
            device_id_type=MESH,
        )

    def add_mirrors(s):
        for i in range(n_cd):
            d = order[i]
            for j in range(n_ab):
                source = mirror_out if j == 0 else mirror_in
                if j:
                    across(j, i).wait_recv()
                for x in range(group):
                    at = pl.ds(d * rows + x * width + near[j] * block, block)
                    partial[s, at] += source[j, pl.ds((d * group + x) * block, block)]
            send_plane(s, i)

    def relay(s):
        @pl.when(inner)
        def _():
            from_plane(s, 3).wait_recv()
            relayed[s] = partial[s, pl.ds(order[2] * rows, rows)] + z_in[s, 3]
            passed_on(s).start()

    def total(s, into):
        from_plane(s, 0).wait_recv()
        from_plane(s, 1).wait_recv()
        into[s] = partial[s, pl.ds(me_cd * rows, rows)] + z_in[s, 0] + z_in[s, 1]

        @pl.when(outer)
        def _():
            from_plane(s, 2).wait_recv()
            into[s] += z_in[s, 2]

    def mirror_copy(s, j, m):
        q = lax.rem(me_cd + m, n_cd)
        return pltpu.make_async_remote_copy(
            src_ref=outgoing.at[s, pl.ds((near[j] * n_cd + q) * piece, piece)],
            dst_ref=mirrored.at[s, pl.ds(own_place * piece, piece)],
            send_sem=mi_send.at[s, j, m],
            recv_sem=mi_recv.at[s, j, m],
            device_id=(near[j], q, me_ij),
            device_id_type=MESH,
        )

    def mirror_arrival(s, j, m):
        place = near[j] * n_cd + lax.rem(me_cd - m + n_cd, n_cd)
        return pltpu.make_async_remote_copy(
            src_ref=outgoing.at[s, pl.ds(0, piece)],
            dst_ref=mirrored.at[s, pl.ds(place * piece, piece)],
            send_sem=mi_send.at[s, j, m],
            recv_sem=mi_recv.at[s, j, m],
            device_id=(near[j], lax.rem(me_cd + m, n_cd), me_ij),
            device_id_type=MESH,
        )

    others = [(j, m) for j in (3, 1, 2, 0) for m in (2, 3, 1, 0) if j or m]

    def send_mirrors(s):
        for x in range(group):
            for y in range(group):
                outgoing[s, pl.ds(x * group + y, targets, stride=piece), :] = pltpu.roll(
                    summed[s, pl.ds(x * width + y, targets, stride=group), :], half, 1
                )
        for j, m in others:
            mirror_copy(s, j, m).start()
        here = pl.ds(own_place * piece, piece)
        mirrored[s, here] = outgoing[s, here]

    def take_mirrors(s):
        for j, m in others:
            mirror_arrival(s, j, m).wait_recv()
        for y in range(group):
            at = pl.ds(y * width, width)
            result[s, at] = summed[s, at] + mirrored[s, pl.ds(y, width, stride=group), :]

    def trade(s):
        return pltpu.make_async_remote_copy(
            src_ref=result.at[s],
            dst_ref=traded.at[s],
            send_sem=tr_send.at[s],
            recv_sem=tr_recv.at[s],
            device_id=(me_ab, me_cd, 1 - me_ij),
            device_id_type=MESH,
        )

    def store(s):
        trade(s).wait_recv()
        lane = lax.broadcasted_iota(jnp.int32, (width, LANES), 1)
        mine = (lane >= half) == (me_ij == 1)
        for y in range(group):
            at = pl.ds(y * width, width)
            out_ref[y, :, pl.ds(s * LANES, LANES)] = jnp.where(
                mine, result[s, at], pltpu.roll(traded[s, at], half, 1)
            )

    last = steps - 1
    for s in range(last):
        gather(s)
        compute(s, True)
        relay(s)
    gather(last)
    compute(last, False)
    for i in range(n_cd):
        for j in (3, 1, 2):
            across(j, i).start()
    for s in range(last):
        total(s, summed)
        send_mirrors(s)
    add_mirrors(last)
    relay(last)
    for s in range(last):
        take_mirrors(s)
        trade(s).start()
    for s in range(last):
        store(s)
    total(last, result)
    trade(last).start()
    store(last)
    for s in range(steps):
        trade(s).wait_send()
        for core in range(2):
            for j in range(1, n_ab):
                spread(s, core, j).wait_send()

            @pl.when(me_ij != core)
            def _():
                spread(s, core, 0).wait_send()

        for i in range(3):
            to_plane(s, i).wait_send()
    for i in range(n_cd):
        for j in range(1, n_ab):
            across(j, i).wait_send()
    for s in range(last):
        for j, m in others:
            mirror_copy(s, j, m).wait_send()


def fused(amplitudes, integrals, tile_row, tile_col, tile_count):
    occ_dev = amplitudes.shape[0]
    slots, size = integrals.shape[0], integrals.shape[1]
    block = math.isqrt(size)
    n_ab, n_cd = lax.axis_size("ab"), lax.axis_size("cd")
    group = block // n_cd
    rows = group * n_ab * block
    steps = occ_dev // LANES
    targets = n_ab * n_cd
    piece = group * group
    f32, bf16 = jnp.float32, jnp.bfloat16
    dma = pltpu.SemaphoreType.DMA
    out = pl.pallas_call(
        functools.partial(ladder_kernel, n_ab, n_cd, block),
        out_shape=jax.ShapeDtypeStruct((group, n_ab * block, occ_dev), f32),
        in_specs=[pl.BlockSpec(memory_space=pltpu.SMEM)] * 3
        + [pl.BlockSpec(memory_space=pl.ANY)] * 2,
        out_specs=pl.BlockSpec(memory_space=pltpu.VMEM),
        scratch_shapes=[
            pltpu.VMEM((slots, size, size), f32),
            pltpu.VMEM((block, n_ab * block, n_ab * size), bf16),
            pltpu.VMEM((block, n_ab * block, n_ab * size), bf16),
            pltpu.VMEM((steps, n_ab, LANES, size), f32),
            pltpu.VMEM((2 * LANES, n_ab * size), bf16),
            pltpu.VMEM((steps, n_cd * rows, LANES), f32),
            pltpu.VMEM((n_ab, size, LANES), f32),
            pltpu.VMEM((n_ab, size, LANES), f32),
            pltpu.VMEM((steps, 4, rows, LANES), f32),
            pltpu.VMEM((steps, rows, LANES), f32),
            pltpu.VMEM((steps, rows, LANES), f32),
            pltpu.VMEM((steps, targets * piece, LANES), f32),
            pltpu.VMEM((steps, targets * piece, LANES), f32),
            pltpu.VMEM((steps, rows, LANES), f32),
            pltpu.VMEM((steps, rows, LANES), f32),
            dma((slots,)),
            dma((steps,)),
            dma((steps, 2, n_ab)),
            dma((steps, n_ab, 2)),
            dma((n_ab, n_cd)),
            dma((n_ab, n_cd)),
            dma((steps, 3)),
            dma((steps, 4)),
            dma((steps, n_ab, n_cd)),
            dma((steps, n_ab, n_cd)),
            dma((steps,)),
            dma((steps,)),
        ],
        compiler_params=pltpu.CompilerParams(
            collective_id=0, has_side_effects=True, vmem_limit_bytes=VMEM_BYTES
        ),
    )(tile_row, tile_col, tile_count, amplitudes, integrals)
    return jnp.transpose(out, (2, 0, 1))[:, None]


def from_partner(block, axis, bit):
    count = lax.axis_size(axis)
    route = []
    for low in range(count):
        high = low | 1 << bit
        if high != low and high < count:
            route += [(low, high), (high, low)]
    return lax.ppermute(block, axis, route)


def place_rows(chosen, tile_rows, row_picks, block_size):
    terms = jnp.einsum("okf,kef->oke", chosen, tile_rows, precision=lax.Precision.HIGHEST)
    occ_dev, slots, width = terms.shape
    terms = terms.reshape(occ_dev, slots, width // block_size, block_size)
    placed = jnp.einsum("rk,okab->aorb", row_picks, terms, precision=lax.Precision.HIGHEST)
    return placed.reshape(width // block_size, occ_dev, row_picks.shape[0] * block_size)


def general(amplitudes, integrals, tile_row, tile_col, tile_count):
    occ_dev = amplitudes.shape[0]
    slots = integrals.shape[0]
    tile_size = integrals.shape[1]
    block_size = math.isqrt(tile_size)
    blocks = lax.axis_size("ab")
    cd_size = lax.axis_size("cd")
    group_size = block_size // cd_size
    live_count = tile_count[0]
    live = jnp.arange(slots, dtype=jnp.int32) < live_count
    row_picks = (
        (tile_row[None, :] == jnp.arange(blocks, dtype=jnp.int32)[:, None]) & live[None, :]
    ).astype(jnp.float32)
    gathered = lax.all_gather(amplitudes, "ab", axis=1, tiled=True)
    columns = gathered.reshape(occ_dev, -1, tile_size)
    chosen = jnp.take(columns, tile_col, axis=1)
    partial_value = place_rows(chosen, integrals, row_picks, block_size)
    summed = lax.psum_scatter(partial_value, "cd", scatter_dimension=0, tiled=True)
    direct = jnp.transpose(summed, (1, 0, 2))
    outgoing = summed.reshape(group_size, occ_dev, blocks, cd_size, group_size)
    outgoing = jnp.transpose(outgoing, (2, 3, 1, 0, 4))
    arrived = lax.all_to_all(
        outgoing.reshape(blocks * cd_size, occ_dev * group_size * group_size),
        ("ab", "cd"),
        split_axis=0,
        concat_axis=0,
        tiled=True,
    )
    arrived = arrived.reshape(blocks, cd_size, occ_dev, group_size, group_size)
    mirrored = jnp.transpose(arrived, (2, 4, 0, 1, 3)).reshape(
        occ_dev, group_size, blocks * block_size
    )
    partner = from_partner(mirrored, "ij", 0)
    return (direct + partner).reshape(occ_dev, 1, group_size, blocks * block_size)


def per_device(amplitudes, integrals, tile_row, tile_col, tile_count):
    n_ab = lax.axis_size("ab")
    if (
        amplitudes.shape[1] == integrals.shape[1]
        and integrals.shape[0] == n_ab * n_ab
        and n_ab == 4
        and lax.axis_size("cd") == 4
        and lax.axis_size("ij") == 2
        and amplitudes.shape[0] % LANES == 0
    ):
        return fused(amplitudes, integrals, tile_row, tile_col, tile_count)
    return general(amplitudes, integrals, tile_row, tile_col, tile_count)


def solution(mesh):
    in_specs = (
        P("ij", ("cd", "ab")),
        P(("ab", "cd"), None, None),
        P(("ab", "cd")),
        P(("ab", "cd")),
        P(("ab", "cd")),
    )
    out_specs = P("ij", "ab", "cd", None)
    return jax.shard_map(
        per_device, mesh=mesh, in_specs=in_specs, out_specs=out_specs, check_vma=False
    )
```

```python
import functools
import math

import jax
import jax.numpy as jnp
from jax import lax
from jax.experimental import pallas as pl
from jax.experimental.pallas import tpu as pltpu
from jax.sharding import PartitionSpec as P

MESH = pl.DeviceIdType.MESH
LANES = 128
VMEM_BYTES = 54848 * 1024


def split(value):
    high = value.astype(jnp.bfloat16)
    low = (value - high.astype(jnp.float32)).astype(jnp.bfloat16)
    return high, low


def ladder_kernel(
    n_ab, n_cd, block,
    key_ref, amp_ref, tiles_ref, out_ref,
    tiles, w_high, w_low, gathered, a_both, partial, mirror_out, mirror_in, z_in, relayed,
    summed, outgoing, mirrored, result, traded,
    tile_sem, own_sem, ag_send, ag_recv, x_send, x_recv, z_send, z_recv,
    mi_send, mi_recv, tr_send, tr_recv,
):
    me_ab, me_cd, me_ij = lax.axis_index("ab"), lax.axis_index("cd"), lax.axis_index("ij")
    slots, size = tiles_ref.shape[0], tiles_ref.shape[1]
    steps = partial.shape[0]
    half = LANES // 2
    group = block // n_cd
    width = n_ab * block
    rows = group * width
    targets = n_ab * n_cd
    piece = group * group
    own_place = me_ab * n_cd + me_cd
    near = [me_ab, me_ab + 1 - 2 * lax.rem(me_ab, 2), lax.rem(me_ab + 2, n_ab), n_ab - 1 - me_ab]
    low_side = me_cd < n_cd // 2
    outer = (me_cd == 0) | (me_cd == n_cd - 1)
    inner = (me_cd > 0) & (me_cd < n_cd - 1)
    far = jnp.where(low_side, n_cd - 1, 0)
    next_in = jnp.where(low_side, 1, 2)
    order = [
        jnp.where(outer, n_cd - 1 - next_in, far),
        jnp.where(outer, far, n_cd - 1 - far),
        jnp.where(outer, next_in, n_cd - 1 - me_cd),
        me_cd,
    ]
    z_device = [
        jnp.where(outer, next_in, far),
        jnp.where(outer, far, n_cd - 1 - far),
        jnp.where(outer, next_in, n_cd - 1 - me_cd),
    ]
    z_slot = [jnp.where(outer, 3, 2), jnp.where(outer, 0, 1), jnp.where(outer, 0, 1)]

    tile_copies = [
        pltpu.make_async_copy(tiles_ref.at[k], tiles.at[k], tile_sem.at[k]) for k in range(slots)
    ]
    for copy in tile_copies:
        copy.start()

    barrier = pltpu.get_barrier_semaphore()
    for j in range(1, n_ab):
        for core in range(2):
            pl.semaphore_signal(
                barrier, inc=1, device_id=(near[j], me_cd, core), device_id_type=MESH
            )
    pl.semaphore_signal(barrier, inc=1, device_id=(me_ab, me_cd, 1 - me_ij), device_id_type=MESH)
    for m in range(1, n_cd):
        pl.semaphore_signal(
            barrier, inc=1, device_id=(me_ab, lax.rem(me_cd + m, n_cd), me_ij), device_id_type=MESH
        )
    pl.semaphore_wait(barrier, 2 * (n_ab - 1) + 1 + n_cd - 1)

    def spread(s, core, j):
        return pltpu.make_async_remote_copy(
            src_ref=amp_ref.at[pl.ds((2 * s + core) * half, half)],
            dst_ref=gathered.at[s, j, pl.ds(me_ij * half, half)],
            send_sem=ag_send.at[s, core, j],
            recv_sem=ag_recv.at[s, j, me_ij],
            device_id=(near[j], me_cd, core),
            device_id_type=MESH,
        )

    def arrival(s, j, h):
        return pltpu.make_async_remote_copy(
            src_ref=amp_ref.at[pl.ds(0, half)],
            dst_ref=gathered.at[s, j, pl.ds(h * half, half)],
            send_sem=ag_send.at[s, 0, j],
            recv_sem=ag_recv.at[s, j, h],
            device_id=(near[j], me_cd, me_ij),
            device_id_type=MESH,
        )

    def keep(s, core):
        return pltpu.make_async_copy(
            amp_ref.at[pl.ds((2 * s + core) * half, half)],
            gathered.at[s, 0, pl.ds(core * half, half)],
            own_sem.at[s],
        )

    for s in range(steps):
        for core in range(2):
            for j in (3, 1, 2):
                spread(s, core, j).start()

            @pl.when(me_ij == core)
            def _():
                keep(s, core).start()

            @pl.when(me_ij != core)
            def _():
                spread(s, core, 0).start()

    keys = [key_ref[k] for k in range(slots)]
    for copy in tile_copies:
        copy.wait()
    for j in range(n_ab):
        column = near[j]
        for r in range(n_ab):
            slot = jnp.int32(slots)
            for k in range(slots):
                slot = jnp.where(keys[k] == r * n_ab + column, jnp.int32(k), slot)
            scale = jnp.where(slot < slots, jnp.float32(1), jnp.float32(0))
            high, low = split(tiles[jnp.minimum(slot, slots - 1)] * scale)
            at = (slice(None), pl.ds(r * block, block), pl.ds(j * size, size))
            w_high[at] = high.reshape(block, block, size)
            w_low[at] = low.reshape(block, block, size)

    contract = (((1,), (1,)), ((), ()))

    def to_plane(s, i):
        source = partial.at[s, pl.ds(order[i] * rows, rows)]
        return pltpu.make_async_remote_copy(
            src_ref=source,
            dst_ref=z_in.at[s, z_slot[i]],
            send_sem=z_send.at[s, i],
            recv_sem=z_recv.at[s, z_slot[i]],
            device_id=(me_ab, z_device[i], me_ij),
            device_id_type=MESH,
        )

    def passed_on(s):
        return pltpu.make_async_remote_copy(
            src_ref=relayed.at[s],
            dst_ref=z_in.at[s, 1],
            send_sem=z_send.at[s, 2],
            recv_sem=z_recv.at[s, 1],
            device_id=(me_ab, z_device[2], me_ij),
            device_id_type=MESH,
        )

    def from_plane(s, place):
        return pltpu.make_async_remote_copy(
            src_ref=relayed.at[s],
            dst_ref=z_in.at[s, place],
            send_sem=z_send.at[s, 0],
            recv_sem=z_recv.at[s, place],
            device_id=(me_ab, z_device[0], me_ij),
            device_id_type=MESH,
        )

    def send_plane(s, i):
        if i < 2:
            to_plane(s, i).start()
        elif i == 2:

            @pl.when(outer)
            def _():
                to_plane(s, i).start()

    def gather(s):
        for j in range(n_ab):
            if j:
                arrival(s, j, 0).wait_recv()
                arrival(s, j, 1).wait_recv()
            else:

                @pl.when(me_ij == 0)
                def _():
                    keep(s, 0).wait()
                    arrival(s, 0, 1).wait_recv()

                @pl.when(me_ij == 1)
                def _():
                    keep(s, 1).wait()
                    arrival(s, 0, 0).wait_recv()

            high, low = split(gathered[s, j])
            a_both[pl.ds(0, LANES), pl.ds(j * size, size)] = high
            a_both[pl.ds(LANES, LANES), pl.ds(j * size, size)] = low

    def compute(s, send):
        for i in range(n_cd):
            d = order[i]
            lead = pl.ds(d * group, group)
            left_high = w_high[lead].reshape(rows, n_ab * size)
            left_low = w_low[lead].reshape(rows, n_ab * size)
            right = a_both[...]
            wide = lax.dot_general(left_high, right, contract, preferred_element_type=jnp.float32)
            value = wide[:, LANES:] + lax.dot_general(
                left_low, right[:LANES], contract, preferred_element_type=jnp.float32
            )
            value += wide[:, :LANES]
            partial[s, pl.ds(d * rows, rows)] = value
            if send:
                send_plane(s, i)
            else:
                for j in range(n_ab):
                    for x in range(group):
                        mirror_out[j, pl.ds(d * group + x, block, stride=block), :] = pltpu.roll(
                            partial[s, pl.ds(d * rows + x * width + near[j] * block, block)], half, 1
                        )

    def across(j, i):
        part = pl.ds(order[i] * group * block, group * block)
        return pltpu.make_async_remote_copy(
            src_ref=mirror_out.at[j, part],
            dst_ref=mirror_in.at[j, part],
            send_sem=x_send.at[j, i],
            recv_sem=x_recv.at[j, i],
            device_id=(near[j], me_cd, me_ij),
            device_id_type=MESH,
        )

    def add_mirrors(s):
        for i in range(n_cd):
            d = order[i]
            for j in range(n_ab):
                source = mirror_out if j == 0 else mirror_in
                if j:
                    across(j, i).wait_recv()
                for x in range(group):
                    at = pl.ds(d * rows + x * width + near[j] * block, block)
                    partial[s, at] += source[j, pl.ds((d * group + x) * block, block)]
            send_plane(s, i)

    def relay(s):
        @pl.when(inner)
        def _():
            from_plane(s, 3).wait_recv()
            relayed[s] = partial[s, pl.ds(order[2] * rows, rows)] + z_in[s, 3]
            passed_on(s).start()

    def total(s, into):
        from_plane(s, 0).wait_recv()
        from_plane(s, 1).wait_recv()
        into[s] = partial[s, pl.ds(me_cd * rows, rows)] + z_in[s, 0] + z_in[s, 1]

        @pl.when(outer)
        def _():
            from_plane(s, 2).wait_recv()
            into[s] += z_in[s, 2]

    def mirror_copy(s, j, m):
        q = lax.rem(me_cd + m, n_cd)
        return pltpu.make_async_remote_copy(
            src_ref=outgoing.at[s, pl.ds((near[j] * n_cd + q) * piece, piece)],
            dst_ref=mirrored.at[s, pl.ds(own_place * piece, piece)],
            send_sem=mi_send.at[s, j, m],
            recv_sem=mi_recv.at[s, j, m],
            device_id=(near[j], q, me_ij),
            device_id_type=MESH,
        )

    def mirror_arrival(s, j, m):
        place = near[j] * n_cd + lax.rem(me_cd - m + n_cd, n_cd)
        return pltpu.make_async_remote_copy(
            src_ref=outgoing.at[s, pl.ds(0, piece)],
            dst_ref=mirrored.at[s, pl.ds(place * piece, piece)],
            send_sem=mi_send.at[s, j, m],
            recv_sem=mi_recv.at[s, j, m],
            device_id=(near[j], lax.rem(me_cd + m, n_cd), me_ij),
            device_id_type=MESH,
        )

    others = [(j, m) for j in (3, 1, 2, 0) for m in (2, 3, 1, 0) if j or m]

    def send_mirrors(s):
        for x in range(group):
            for y in range(group):
                outgoing[s, pl.ds(x * group + y, targets, stride=piece), :] = pltpu.roll(
                    summed[s, pl.ds(x * width + y, targets, stride=group), :], half, 1
                )
        for j, m in others:
            mirror_copy(s, j, m).start()
        here = pl.ds(own_place * piece, piece)
        mirrored[s, here] = outgoing[s, here]

    def take_mirrors(s):
        for j, m in others:
            mirror_arrival(s, j, m).wait_recv()
        for y in range(group):
            at = pl.ds(y * width, width)
            result[s, at] = summed[s, at] + mirrored[s, pl.ds(y, width, stride=group), :]

    def trade(s):
        return pltpu.make_async_remote_copy(
            src_ref=result.at[s],
            dst_ref=traded.at[s],
            send_sem=tr_send.at[s],
            recv_sem=tr_recv.at[s],
            device_id=(me_ab, me_cd, 1 - me_ij),
            device_id_type=MESH,
        )

    def store(s):
        trade(s).wait_recv()
        lane = lax.broadcasted_iota(jnp.int32, (width, LANES), 1)
        mine = (lane >= half) == (me_ij == 1)
        for y in range(group):
            at = pl.ds(y * width, width)
            out_ref[y, :, pl.ds(s * LANES, LANES)] = jnp.where(
                mine, result[s, at], pltpu.roll(traded[s, at], half, 1)
            )

    last = steps - 1
    for s in range(last):
        gather(s)
        compute(s, True)
        relay(s)
    gather(last)
    compute(last, False)
    for i in range(n_cd):
        for j in (3, 1, 2):
            across(j, i).start()
    for s in range(last):
        total(s, summed)
        send_mirrors(s)
    add_mirrors(last)
    relay(last)
    for s in range(last):
        take_mirrors(s)
        trade(s).start()
    for s in range(last):
        store(s)
    total(last, result)
    trade(last).start()
    store(last)
    for s in range(steps):
        trade(s).wait_send()
        for core in range(2):
            for j in range(1, n_ab):
                spread(s, core, j).wait_send()

            @pl.when(me_ij != core)
            def _():
                spread(s, core, 0).wait_send()

        for i in range(3):
            to_plane(s, i).wait_send()
    for i in range(n_cd):
        for j in range(1, n_ab):
            across(j, i).wait_send()
    for s in range(last):
        for j, m in others:
            mirror_copy(s, j, m).wait_send()


def fused(amplitudes, integrals, tile_row, tile_col, tile_count):
    occ_dev = amplitudes.shape[0]
    slots, size = integrals.shape[0], integrals.shape[1]
    block = math.isqrt(size)
    n_ab, n_cd = lax.axis_size("ab"), lax.axis_size("cd")
    group = block // n_cd
    rows = group * n_ab * block
    steps = occ_dev // LANES
    targets = n_ab * n_cd
    piece = group * group
    f32, bf16 = jnp.float32, jnp.bfloat16
    dma = pltpu.SemaphoreType.DMA
    live = jnp.arange(slots, dtype=jnp.int32) < tile_count[0]
    keys = jnp.where(live, tile_row * n_ab + tile_col, jnp.int32(-1))
    out = pl.pallas_call(
        functools.partial(ladder_kernel, n_ab, n_cd, block),
        out_shape=jax.ShapeDtypeStruct((group, n_ab * block, occ_dev), f32),
        in_specs=[pl.BlockSpec(memory_space=pltpu.SMEM)]
        + [pl.BlockSpec(memory_space=pl.ANY)] * 2,
        out_specs=pl.BlockSpec(memory_space=pltpu.VMEM),
        scratch_shapes=[
            pltpu.VMEM((slots, size, size), f32),
            pltpu.VMEM((block, n_ab * block, n_ab * size), bf16),
            pltpu.VMEM((block, n_ab * block, n_ab * size), bf16),
            pltpu.VMEM((steps, n_ab, LANES, size), f32),
            pltpu.VMEM((2 * LANES, n_ab * size), bf16),
            pltpu.VMEM((steps, n_cd * rows, LANES), f32),
            pltpu.VMEM((n_ab, size, LANES), f32),
            pltpu.VMEM((n_ab, size, LANES), f32),
            pltpu.VMEM((steps, 4, rows, LANES), f32),
            pltpu.VMEM((steps, rows, LANES), f32),
            pltpu.VMEM((steps, rows, LANES), f32),
            pltpu.VMEM((steps, targets * piece, LANES), f32),
            pltpu.VMEM((steps, targets * piece, LANES), f32),
            pltpu.VMEM((steps, rows, LANES), f32),
            pltpu.VMEM((steps, rows, LANES), f32),
            dma((slots,)),
            dma((steps,)),
            dma((steps, 2, n_ab)),
            dma((steps, n_ab, 2)),
            dma((n_ab, n_cd)),
            dma((n_ab, n_cd)),
            dma((steps, 3)),
            dma((steps, 4)),
            dma((steps, n_ab, n_cd)),
            dma((steps, n_ab, n_cd)),
            dma((steps,)),
            dma((steps,)),
        ],
        compiler_params=pltpu.CompilerParams(
            collective_id=0, has_side_effects=True, vmem_limit_bytes=VMEM_BYTES
        ),
    )(keys, amplitudes, integrals)
    return jnp.transpose(out, (2, 0, 1))[:, None]


def from_partner(block, axis, bit):
    count = lax.axis_size(axis)
    route = []
    for low in range(count):
        high = low | 1 << bit
        if high != low and high < count:
            route += [(low, high), (high, low)]
    return lax.ppermute(block, axis, route)


def place_rows(chosen, tile_rows, row_picks, block_size):
    terms = jnp.einsum("okf,kef->oke", chosen, tile_rows, precision=lax.Precision.HIGHEST)
    occ_dev, slots, width = terms.shape
    terms = terms.reshape(occ_dev, slots, width // block_size, block_size)
    placed = jnp.einsum("rk,okab->aorb", row_picks, terms, precision=lax.Precision.HIGHEST)
    return placed.reshape(width // block_size, occ_dev, row_picks.shape[0] * block_size)


def general(amplitudes, integrals, tile_row, tile_col, tile_count):
    occ_dev = amplitudes.shape[0]
    slots = integrals.shape[0]
    tile_size = integrals.shape[1]
    block_size = math.isqrt(tile_size)
    blocks = lax.axis_size("ab")
    cd_size = lax.axis_size("cd")
    group_size = block_size // cd_size
    live_count = tile_count[0]
    live = jnp.arange(slots, dtype=jnp.int32) < live_count
    row_picks = (
        (tile_row[None, :] == jnp.arange(blocks, dtype=jnp.int32)[:, None]) & live[None, :]
    ).astype(jnp.float32)
    gathered = lax.all_gather(amplitudes, "ab", axis=1, tiled=True)
    columns = gathered.reshape(occ_dev, -1, tile_size)
    chosen = jnp.take(columns, tile_col, axis=1)
    partial_value = place_rows(chosen, integrals, row_picks, block_size)
    summed = lax.psum_scatter(partial_value, "cd", scatter_dimension=0, tiled=True)
    direct = jnp.transpose(summed, (1, 0, 2))
    outgoing = summed.reshape(group_size, occ_dev, blocks, cd_size, group_size)
    outgoing = jnp.transpose(outgoing, (2, 3, 1, 0, 4))
    arrived = lax.all_to_all(
        outgoing.reshape(blocks * cd_size, occ_dev * group_size * group_size),
        ("ab", "cd"),
        split_axis=0,
        concat_axis=0,
        tiled=True,
    )
    arrived = arrived.reshape(blocks, cd_size, occ_dev, group_size, group_size)
    mirrored = jnp.transpose(arrived, (2, 4, 0, 1, 3)).reshape(
        occ_dev, group_size, blocks * block_size
    )
    partner = from_partner(mirrored, "ij", 0)
    return (direct + partner).reshape(occ_dev, 1, group_size, blocks * block_size)


def per_device(amplitudes, integrals, tile_row, tile_col, tile_count):
    n_ab = lax.axis_size("ab")
    if (
        amplitudes.shape[1] == integrals.shape[1]
        and integrals.shape[0] == n_ab * n_ab
        and n_ab == 4
        and lax.axis_size("cd") == 4
        and lax.axis_size("ij") == 2
        and amplitudes.shape[0] % LANES == 0
    ):
        return fused(amplitudes, integrals, tile_row, tile_col, tile_count)
    return general(amplitudes, integrals, tile_row, tile_col, tile_count)


def solution(mesh):
    in_specs = (
        P("ij", ("cd", "ab")),
        P(("ab", "cd"), None, None),
        P(("ab", "cd")),
        P(("ab", "cd")),
        P(("ab", "cd")),
    )
    out_specs = P("ij", "ab", "cd", None)
    return jax.shard_map(
        per_device, mesh=mesh, in_specs=in_specs, out_specs=out_specs, check_vma=False
    )
```
